128 devices in a mesh: scen: 8 (over x, z_hi), border: 16 (over y, z_lo, core).
Axes of the slice: x: 4, y: 4, z: 4 (z_hi: 2, z_lo: 2; z = z_hi * 2 + z_lo), core: 2. Of those that a mesh axis runs over, the one named last changes fastest.
Arguments:
- border: bfloat16 [16, 512, 65536], P('scen', None, 'border'), may hold values from -1.5 to 1.5
- blocks: float32 [16, 512, 512], P('scen'), may hold values from -60 to 64, as said below
- root_diag: float32 [65536], P('border'), may hold values from 4 to 128
- live_rows: int32 [16], P('scen'), may hold values from 128 to 512, as said below
- panel_ids: int32 [4], replicated, may hold values from 0 to 255
Outputs:
- root_rows: float32 [16, 4096, 1024], P('border', 'scen')
- factor: float32 [4, 256, 256], replicated
The draws below stay inside these ranges and needn't reach their ends.
Inputs may be any that keep to these rules, and one draw needn't show every extreme that they name: blocks[i] is a Gram matrix plus a positive diagonal of at least 1, hence symmetric positive definite. `live_rows`: each entry is a multiple of 128, and some scenario has 512.
All inputs are finite; a program needn't handle non-finite values.
Results may differ from the reference program's by a relative error of at most 0.0017.
Values may be sent and summed in bfloat16 or wider, within the bound.
No kernel may reach another device: no remote copies, remote signals or barrier semaphores. Data moves between devices by JAX's collectives and lax.ppermute only.
A program may use at most 128 MiB of HBM per device.

```python
import math
import jax
import jax.numpy as jnp
from jax import lax

NS = 512
BCOL = 4096
PW = 256
PANELS = 4
SCEN = 16
NB = 65536
PR = 1024
NPANEL = 256
N_BORDER = 16


def draw_blocks(key, part):
    key_left = jax.random.fold_in(key, 11)
    key_diag = jax.random.fold_in(key, 12)
    key_spike = jax.random.fold_in(key, 13)
    key_scale = jax.random.fold_in(key, 14)
    factors = jax.random.truncated_normal(key_left, -3.0, 3.0, (SCEN, NS, NS), jnp.float32)
    gram = jnp.einsum('ikr,ijr->ikj', factors, factors, precision=lax.Precision.HIGHEST) / NS
    spike_cols = jax.random.uniform(key_spike, (SCEN, NS, 16), jnp.float32, -1.0, 1.0)
    spike_scale = jnp.exp(jax.random.uniform(key_scale, (SCEN, 16), jnp.float32, 0.0, 0.5 * jnp.log(10.0)))
    lifted = spike_cols * spike_scale[:, None, :]
    spikes = 0.3 * jnp.einsum('ikr,ijr->ikj', lifted, lifted, precision=lax.Precision.HIGHEST)
    diagonal = jnp.exp(jax.random.uniform(key_diag, (SCEN, NS), jnp.float32, 0.0, jnp.log(4.0)))
    eye_mat = jnp.eye(NS, dtype=jnp.float32)
    return gram + spikes + diagonal[:, :, None] * eye_mat[None, :, :]


def draw_live_rows(key, part):
    key_count = jax.random.fold_in(key, 21)
    key_full = jax.random.fold_in(key, 22)
    quarter = NS // 4
    counts = jax.random.randint(key_count, (SCEN,), 1, 5, jnp.int32) * quarter
    chosen = jax.random.randint(key_full, (), 0, SCEN, jnp.int32)
    return jnp.where(jnp.arange(SCEN, dtype=jnp.int32) == chosen, jnp.int32(NS), counts).astype(jnp.int32)


def plant(result, own_key, low, high):
    place = [jax.random.randint(jax.random.fold_in(own_key, axis), (), 0, length) for axis, length in enumerate(result.shape)]
    main_axis = result.shape.index(max(result.shape))
    neighbour = place[:main_axis] + [(place[main_axis] + 1) % result.shape[main_axis]] + place[main_axis + 1:]
    return result.at[tuple(place)].set(low).at[tuple(neighbour)].set(high)


def level_of(stream_key, extent, shards, least, largest):
    factor_of, own = 1.0, jax.random.fold_in(stream_key, 6)
    for dim, parts in shards:
        draws = jnp.exp(jax.random.uniform(jax.random.fold_in(own, dim), (parts,), jnp.float32, least / len(shards), largest / len(shards)))
        factor_of = factor_of * jnp.repeat(draws, extent[dim] // parts).reshape([-1 if axis == dim else 1 for axis in range(len(extent))])
    return factor_of


def noise(own_key, shape, scale, bound, pieces=(), kind=jnp.bfloat16):
    factor_of = level_of(own_key, shape, pieces, -0.22, 0.18) if pieces else 1.0
    result = jax.random.normal(own_key, shape, jnp.float32) * scale * factor_of
    return jnp.minimum(jnp.maximum(result, -bound), bound).astype(kind)


def setup_inputs(seed: int = 0) -> dict:
    seeds = jax.random.split(jax.random.key(seed), 6)
    return {
        "border": noise(seeds[0], (SCEN, NS, NB), 0.25, 1.5, ((0, 8), (2, 16))),
        "blocks": draw_blocks(jax.random.fold_in(seeds[5], 71), 0),
        "root_diag": jnp.clip(jnp.exp(math.log(128.0) - 3.465736 * jax.random.uniform(seeds[2], (NB,), jnp.float32) ** level_of(seeds[2], (NB,), ((0, 16),), -0.2, 0.2)), 4.0, 128.0),
        "live_rows": draw_live_rows(jax.random.fold_in(seeds[5], 71), 0),
        "panel_ids": plant(jax.random.randint(seeds[4], (PANELS,), 0, NPANEL), jax.random.fold_in(seeds[4], 1), 0, NPANEL - 1).astype(jnp.int32),
    }


def reference(border, blocks, root_diag, live_rows, panel_ids):
    panel_cols = (panel_ids[:, None] * PW + jnp.arange(PW, dtype=jnp.int32)[None, :]).reshape(-1).astype(jnp.int32)
    levels = jnp.arange(NS, dtype=jnp.int32)
    identity = jnp.eye(NS, dtype=jnp.float32)

    def one_scenario(total, item):
        rows_in, block, live = item
        keep = levels >= NS - live
        masked = jnp.where(keep[:, None], rows_in, jnp.zeros_like(rows_in))
        lower_factor = jnp.linalg.cholesky(block)
        inverse = lax.linalg.triangular_solve(lower_factor, identity, left_side=True, lower=True).astype(jnp.bfloat16)
        solved = jnp.dot(inverse.astype(jnp.float32), masked.astype(jnp.float32), preferred_element_type=jnp.float32).astype(jnp.bfloat16)
        panels = jnp.take(solved, panel_cols, axis=1)
        total = total + jnp.dot(panels.T.astype(jnp.float32), solved.astype(jnp.float32), preferred_element_type=jnp.float32)
        return (total, None)
    schur, unused = lax.scan(one_scenario, jnp.zeros((PR, NB), jnp.float32), (border, blocks, live_rows))
    columns = jnp.arange(NB, dtype=jnp.int32)
    schur = schur + jnp.where(columns[None, :] == panel_cols[:, None], root_diag[None, :], jnp.zeros((), jnp.float32))
    tiles = []
    for position in range(PANELS):
        row_start = jnp.asarray(position * PW, jnp.int32)
        col_start = (panel_ids[position] * PW).astype(jnp.int32)
        tiles.append(lax.dynamic_slice(schur, (row_start, col_start), (PW, PW)))
    diag_block = jnp.stack(tiles)
    factor = jnp.linalg.cholesky(diag_block)
    eye_stack = jnp.broadcast_to(jnp.eye(PW, dtype=jnp.float32), diag_block.shape)
    factor_inverse = lax.linalg.triangular_solve(factor, eye_stack, left_side=True, lower=True)
    solved_rows = jnp.einsum('pkj,pjc->pkc', factor_inverse, schur.reshape(PANELS, PW, NB), precision=lax.Precision.HIGHEST)
    root_rows = solved_rows.reshape(PR, N_BORDER, BCOL).transpose(1, 2, 0)
    return (root_rows, factor)
```

```python
import functools

import jax
import jax.numpy as jnp
from jax import lax
from jax.experimental import pallas as pl
from jax.experimental.pallas import tpu as pltpu
from jax.sharding import PartitionSpec as P


HI = lax.Precision.HIGHEST
F32, BF16, F16 = jnp.float32, jnp.bfloat16, jnp.float16
LB = 128
STEP = 16
PW = 256
PANELS = 4
EXTRA = 16
VM = pl.BlockSpec(memory_space=pltpu.VMEM)
SM = pl.BlockSpec(memory_space=pltpu.SMEM)
ANY = pl.BlockSpec(memory_space=pl.ANY)
LIMIT = 60 << 20


def params(**kw):
    return pltpu.CompilerParams(vmem_limit_bytes=LIMIT, **kw)


def cost(us):
    return pl.CostEstimate(flops=int(us * 1.0e9), bytes_accessed=1 << 20, transcendentals=0)


def eliminate(mats):
    rows = lax.broadcasted_iota(jnp.int32, (STEP, LB), 0)
    for r0 in range(0, LB, STEP):
        panels = [m[r0 : r0 + STEP, :] for m in mats]
        cols = [
            [jnp.broadcast_to(r[:, r0 + j : r0 + j + 1], (STEP, LB)) for j in range(STEP)]
            for r in panels
        ]
        pivots = [jnp.ones((STEP, LB), F32) for _ in mats]
        for j in range(STEP):
            for b in range(len(mats)):
                c = cols[b]
                pivot = jnp.broadcast_to(c[j][j : j + 1, :], (STEP, LB))
                pivots[b] = jnp.where(rows == j, pivot, pivots[b])
                if j == STEP - 1:
                    continue
                mult = jnp.where(rows > j, c[j] / pivot, 0.0)
                for k in range(j + 1, STEP):
                    c[k] = c[k] - mult * jnp.broadcast_to(c[k][j : j + 1, :], (STEP, LB))
                both = jnp.concatenate([mult, mult], axis=1)
                panels[b] = panels[b] - both * jnp.broadcast_to(
                    panels[b][j : j + 1, :], (STEP, 2 * LB)
                )
        for b, m in enumerate(mats):
            s = lax.rsqrt(pivots[b])
            done = panels[b] * jnp.concatenate([s, s], axis=1)
            m[r0 : r0 + STEP, :] = done
            if r0 + STEP < LB:
                upd = lax.dot_general(
                    done[:, :LB], done, (((0,), (0,)), ((), ())),
                    precision=HI, preferred_element_type=F32,
                )
                m[r0 + STEP :, :] = m[r0 + STEP :, :] - upd[r0 + STEP :, :]


def factor_step(k, batch, n, g, leafs, u_ref):
    ri = lax.broadcasted_iota(jnp.int32, (LB, LB), 0)
    ci = lax.broadcasted_iota(jnp.int32, (LB, LB), 1)
    eye = (ri == ci).astype(F32)
    own = slice(k * LB, (k + 1) * LB)
    for b in range(batch):
        leafs[b, :, :LB] = g[b, own, own]
        leafs[b, :, LB:] = eye
    eliminate([leafs.at[b] for b in range(batch)])
    for b in range(batch):
        xk = jnp.where(ri >= ci, leafs[b, :, LB:], 0.0)
        w = jnp.dot(xk, g[b, own, :], precision=HI, preferred_element_type=F32)
        if u_ref is not None:
            u_ref[b, own, :] = w
            u_ref[b, own, own] = jnp.where(ri <= ci, leafs[b, :, :LB], 0.0)
        g[b, own, :] = w
        g[b, own, own] = xk
    for b in range(batch):
        for i in range(k + 1, n // LB):
            below = slice(i * LB, (i + 1) * LB)
            upd = lax.dot_general(
                g[b, own, below], g[b, own, :], (((0,), (0,)), ((), ())),
                precision=HI, preferred_element_type=F32,
            )
            g[b, below, own] = jnp.zeros((LB, LB), F32)
            g[b, below, :] = g[b, below, :] - upd


def lower_inverse(g, b, n):
    rr = lax.broadcasted_iota(jnp.int32, (n, n), 0)
    cc = lax.broadcasted_iota(jnp.int32, (n, n), 1)
    return jnp.where(rr >= cc, g[b], 0.0)


def block_inverse_kernel(a_ref, x_ref, g, leafs):
    batch, n, _ = a_ref.shape
    g[...] = a_ref[...]
    for k in range(n // LB):
        factor_step(k, batch, n, g, leafs, None)
    for b in range(batch):
        x_ref[b] = lower_inverse(g, b, n).astype(x_ref.dtype)


def block_inverse(a):
    return pl.pallas_call(
        block_inverse_kernel,
        out_shape=jax.ShapeDtypeStruct(a.shape, BF16),
        in_specs=[VM],
        out_specs=VM,
        scratch_shapes=[pltpu.VMEM(a.shape, F32), pltpu.VMEM((a.shape[0], LB, 2 * LB), F32)],
        compiler_params=params(),
        cost_estimate=cost(28),
        name="block_inverse",
    )(a)


def root_factor_kernel(own_ref, other_ref, diag_ref, u_ref, x_ref, g, leafs):
    batch, n, _ = u_ref.shape
    pos = lax.axis_index("border")
    y, core = pos // 4, pos % 2
    for d in range(PANELS):
        p = (y + PANELS - d) % PANELS
        g[p, pl.ds(pl.multiple_of(core * LB, LB), LB), :] = own_ref[d]
        g[p, pl.ds(pl.multiple_of((1 - core) * LB, LB), LB), :] = other_ref[d]
    rr = lax.broadcasted_iota(jnp.int32, (n, n), 0)
    cc = lax.broadcasted_iota(jnp.int32, (n, n), 1)
    for p in range(batch):
        g[p] = g[p] + jnp.where(rr == cc, jnp.broadcast_to(diag_ref[p : p + 1, :], (n, n)), 0.0)
    for k in range(n // LB):
        factor_step(k, batch, n, g, leafs, u_ref)
    for p in range(batch):
        x_ref[p] = lower_inverse(g, p, n)
        u_ref[p] = jnp.where(rr <= cc, u_ref[p], 0.0)


def root_factor(own, other, diag):
    shape = (PANELS, PW, PW)
    return pl.pallas_call(
        root_factor_kernel,
        out_shape=[jax.ShapeDtypeStruct(shape, F32)] * 2,
        in_specs=[VM, VM, VM],
        out_specs=[VM, VM],
        scratch_shapes=[pltpu.VMEM(shape, F32), pltpu.VMEM((PANELS, LB, 2 * LB), F32)],
        compiler_params=params(),
        cost_estimate=cost(18),
        name="root_factor",
    )(own, other, diag)


def gather_kernel(ids_ref, live_ref, diag_ref, border_ref, send_ref, keep_ref, buf, sems):
    scen_local, order, width = border_ref.shape
    pos = lax.axis_index("border")
    y, core = pos // 4, pos % 2
    slabs = width // PW
    copies, owned, offsets = [], [], []
    for d in range(PANELS):
        chosen = ids_ref[(y + d) % PANELS]
        offset = pl.multiple_of(chosen % slabs * PW, PW)
        owned.append(chosen // slabs == pos)
        offsets.append(offset)
        for i in range(scen_local):
            copy = pltpu.make_async_copy(
                border_ref.at[i, :, pl.ds(offset, PW)], buf.at[d, i], sems.at[d, i]
            )
            copy.start()
            copies.append(copy)
    for copy in copies:
        copy.wait()
    rows = lax.broadcasted_iota(jnp.int32, (order, PW), 0)
    extra = lax.broadcasted_iota(jnp.int32, (EXTRA, PW), 0)
    for d in range(PANELS):
        full = diag_ref[:, pl.ds(offsets[d], PW)]
        high = full.astype(BF16).astype(F32)
        mid = (full - high).astype(BF16).astype(F32)
        low = full - high - mid
        tail = jnp.where(extra == 0, high, jnp.where(extra == 1, mid, jnp.where(extra == 2, low, 0.0)))
        tail = jnp.where(owned[d], tail, 0.0).astype(BF16)
        for ref, i in ((send_ref, 1 - core), (keep_ref, core)):
            first = jnp.where(owned[d], order - live_ref[i], order)
            block = buf[d, i].astype(F32)
            ref[d, :order, :] = jnp.where(rows >= first, block, 0.0).astype(BF16)
            ref[d, order:, :] = tail


def gather(panel_ids, live_rows, root_diag, border):
    scen_local, order, width = border.shape
    shape = jax.ShapeDtypeStruct((PANELS, order + EXTRA, PW), BF16)
    return pl.pallas_call(
        gather_kernel,
        out_shape=[shape, shape],
        in_specs=[SM, SM, VM, ANY],
        out_specs=[VM, VM],
        scratch_shapes=[
            pltpu.VMEM((PANELS, scen_local, order, PW), BF16),
            pltpu.SemaphoreType.DMA((PANELS, scen_local)),
        ],
        compiler_params=params(),
        cost_estimate=cost(3),
        name="gather_window",
    )(panel_ids, live_rows, root_diag.reshape(1, width), border)


def panel_kernel(x_ref, own_ref, other_ref, lo_ref, hi_ref, part_ref, diag_ref, mine):
    order = x_ref.shape[1]
    pos = lax.axis_index("border")
    y, core = pos // 4, pos % 2
    for d in range(PANELS):
        p = (y + PANELS - d) % PANELS
        tail = own_ref[d, order:, :].astype(F32)
        diag_ref[pl.ds(p, 1), :] = tail[0:1] + tail[1:2] + tail[2:3]
        for ref, i in ((own_ref, core), (other_ref, 1 - core)):
            block = jnp.dot(
                x_ref[i], ref[d, :order, :], preferred_element_type=F32
            ).astype(BF16)
            rows = pl.ds(pl.multiple_of(i * order, order), order)
            cols = pl.ds(pl.multiple_of(p % 2 * PW, PW), PW)

            @pl.when(p < 2)
            def _():
                lo_ref[rows, cols] = block

            @pl.when(p >= 2)
            def _():
                hi_ref[rows, cols] = block

            if d == 0:
                mine[rows, :] = block
    full = lax.dot_general(
        mine[...], mine[...], (((0,), (0,)), ((), ())), preferred_element_type=F32
    )
    part_ref[...] = jnp.where(core == 0, full[:LB], full[LB:])


def window_panels(inverse, own, other):
    scen_local, order, _ = inverse.shape
    deep = scen_local * order
    return pl.pallas_call(
        panel_kernel,
        out_shape=[
            jax.ShapeDtypeStruct((deep, 2 * PW), BF16),
            jax.ShapeDtypeStruct((deep, 2 * PW), BF16),
            jax.ShapeDtypeStruct((LB, PW), F32),
            jax.ShapeDtypeStruct((PANELS, PW), F32),
        ],
        in_specs=[VM, VM, VM],
        out_specs=[VM] * 4,
        scratch_shapes=[pltpu.VMEM((deep, PW), BF16)],
        compiler_params=params(),
        cost_estimate=cost(3),
        name="window_panels",
    )(inverse, own, other)


def solve_kernel(order_ref, live_ref, x_ref, b_ref, o_ref):
    n = x_ref.shape[1]
    i = pl.program_id(1)
    rows = lax.broadcasted_iota(jnp.int32, b_ref.shape[1:], 0)
    masked = jnp.where(rows >= n - live_ref[i], b_ref[0].astype(F32), 0.0).astype(BF16)
    o_ref[0] = jnp.dot(x_ref[i], masked, preferred_element_type=F32).astype(BF16)


def solve(dests, live_rows, inverse, border):
    scen_local, n, width = border.shape
    blocks = dests.shape[0]
    share = width // blocks
    return pl.pallas_call(
        solve_kernel,
        out_shape=jax.ShapeDtypeStruct((blocks, scen_local * n, share), BF16),
        grid_spec=pltpu.PrefetchScalarGridSpec(
            num_scalar_prefetch=2,
            grid=(blocks, scen_local),
            in_specs=[
                pl.BlockSpec((scen_local, n, n), lambda j, i, o, l: (0, 0, 0)),
                pl.BlockSpec((1, n, share), lambda j, i, o, l: (i, 0, o[j])),
            ],
            out_specs=pl.BlockSpec((1, n, share), lambda j, i, o, l: (j, i, 0)),
        ),
        compiler_params=params(),
        cost_estimate=cost(10),
        name="solve_border",
    )(dests, live_rows, inverse, border)


def apply_kernel(lo_ref, hi_ref, x_ref, o_ref):
    for p in range(PANELS):
        ref = lo_ref if p < 2 else hi_ref
        cols = slice(p % 2 * PW, (p % 2 + 1) * PW)
        o_ref[:, p * PW : (p + 1) * PW] = lax.dot_general(
            ref[:, cols], x_ref[p], (((1,), (1,)), ((), ())),
            precision=HI, preferred_element_type=F32,
        )


def apply_inverse(lo, hi, factor_inverse):
    return pl.pallas_call(
        apply_kernel,
        out_shape=jax.ShapeDtypeStruct((lo.shape[0], PANELS * PW), F32),
        in_specs=[VM, VM, VM],
        out_specs=VM,
        compiler_params=params(),
        cost_estimate=cost(4),
        name="apply_inverse",
    )(lo, hi, factor_inverse)


def border_move(value, dy=0, dz=0, dc=0):
    pairs = [
        ((y * 2 + z) * 2 + c, (((y + dy) % 4) * 2 + (z ^ dz)) * 2 + (c ^ dc))
        for y in range(4)
        for z in range(2)
        for c in range(2)
    ]
    return lax.ppermute(value, "border", pairs)


def scen_move(value, dx=0, dz=0, flip=0):
    pairs = [
        (x * 2 + z, (((x + dx) % 4) ^ flip) * 2 + (z ^ dz)) for x in range(4) for z in range(2)
    ]
    return lax.ppermute(value, "scen", pairs)


def gram(blocks, panels, add=None):
    total = jnp.einsum("jkc,kq->jcq", blocks, panels, preferred_element_type=F32)
    return total if add is None else total + add.astype(F32)


def on_device(border, blocks, root_diag, live_rows, panel_ids):
    scen_local, order, width = border.shape
    scen_count = lax.axis_size("scen")
    share = width // scen_count
    border_pos = lax.axis_index("border")
    scen_pos = lax.axis_index("scen")

    send, keep = gather(panel_ids, live_rows, root_diag, border)
    got = border_move(send, dc=1)
    away = [border_move(keep[d] + got[d], dy=d) for d in (1, 2, 3)]
    column = keep[0] + got[0] + away[0] + away[1] + away[2]
    column = column + border_move(column, dz=1)
    others = [border_move(column, dy=d) for d in (1, 2, 3)]
    own = jnp.stack([column, *others])
    other = border_move(own, dc=1)

    inverse = block_inverse(blocks)
    rel_x = jnp.array([2, 1, 3, 0, 2, 1, 3, 0], jnp.int32)
    rel_z = jnp.array([1, 1, 1, 1, 0, 0, 0, 0], jnp.int32)
    my_x, my_z = scen_pos // 2, scen_pos % 2
    dests = (my_x + rel_x) % 4 * 2 + (my_z + rel_z) % 2
    solved = solve(dests, live_rows, inverse, border)
    lo, hi, part, diag = window_panels(inverse, own, other)

    part = part + scen_move(part, dz=1)
    part = part + scen_move(part, flip=1)
    part = part + scen_move(part, dx=2)
    stacked = jnp.stack([part, *(border_move(part, dy=d) for d in (1, 2, 3))])
    upper, factor_inverse = root_factor(stacked, border_move(stacked, dc=1), diag)
    factor = jnp.swapaxes(upper, 1, 2)

    hi_far = scen_move(gram(solved[0:1], hi).astype(F16), dz=1)
    lo_far = gram(solved[0:5:4], lo).astype(F16)
    back_lo = scen_move(lo_far[0], dx=3)
    ahead_lo = scen_move(lo_far[1], dx=1)
    hi_near = scen_move(gram(solved[1:4], hi).astype(F16), dz=1)

    half = share // 2
    hi_two = gram(solved[4:5], hi, hi_far)[0].astype(F16)
    back_hi = scen_move(hi_two[:half], dx=3)
    ahead_hi = scen_move(hi_two[half:], dx=1)

    lo_next = jnp.stack([
        gram(solved[1:2], lo)[0].astype(F16),
        gram(solved[5:6], lo, ahead_lo)[0].astype(F16),
    ])
    lo_prev = jnp.stack([
        gram(solved[2:3], lo, back_lo)[0].astype(F16),
        gram(solved[6:7], lo)[0].astype(F16),
    ])
    from_prev = scen_move(lo_next, dx=1)
    from_next = scen_move(lo_prev, dx=3)
    across = (
        gram(solved[3:4], lo)[0] + from_prev[0].astype(F32) + from_next[0].astype(F32)
    ).astype(F16)
    lo_cross = scen_move(across, dz=1)

    none = jnp.zeros_like(back_hi)
    hi_next = (
        gram(solved[5:6], hi, hi_near[0:1])[0] + jnp.concatenate([none, ahead_hi]).astype(F32)
    ).astype(F16)
    hi_prev = (
        gram(solved[6:7], hi, hi_near[1:2])[0] + jnp.concatenate([back_hi, none]).astype(F32)
    ).astype(F16)
    hi_from_prev = scen_move(hi_next, dx=1)
    hi_from_next = scen_move(hi_prev, dx=3)

    base = border_pos * width + scen_pos * share
    global_cols = base + jnp.arange(share, dtype=jnp.int32)
    window_cols = (panel_ids[:, None] * PW + jnp.arange(PW, dtype=jnp.int32)[None, :]).reshape(-1)
    diag_part = lax.dynamic_slice_in_dim(root_diag, scen_pos * share, share)
    matches = global_cols[:, None] == window_cols[None, :]
    added = jnp.where(matches, diag_part[:, None], jnp.zeros((), F32))
    lo_sum = (
        gram(solved[7:8], lo)[0]
        + added[:, : 2 * PW]
        + from_prev[1].astype(F32)
        + from_next[1].astype(F32)
        + lo_cross.astype(F32)
    )
    hi_sum = (
        gram(solved[7:8], hi, hi_near[2:3])[0]
        + added[:, 2 * PW :]
        + hi_from_prev.astype(F32)
        + hi_from_next.astype(F32)
    )
    rows = apply_inverse(lo_sum, hi_sum, factor_inverse)
    return (rows.reshape(1, share, PANELS * PW), factor)


def solution(mesh):
    placed = (P("scen", None, "border"), P("scen", None, None), P("border"), P("scen"), P())
    return jax.shard_map(
        on_device,
        mesh=mesh,
        in_specs=placed,
        out_specs=(P("border", "scen", None), P()),
        check_vma=False,
    )
```
